32 devices in a mesh: groups: 2 (over y), expert: 16 (over z, x, core), head: 1.
Axes of the slice: x: 2, y: 2, z: 4, core: 2. Of those that a mesh axis runs over, the one named last changes fastest.
Arguments:
- sources: bfloat16 [4096, 1024], P(('groups', 'expert')), parts along dimension 0, may hold values from -6 to 6
- enc_gain: float32 [1024], replicated, may hold values from 0.1 to 1.9
- route_ids: int32 [4096, 2], P(('groups', 'expert')), parts along dimension 0, may hold values from 0 to 7, all different within a row; in each aligned block of 128 rows (0 to 127, 128 to 255, ...) at most 40 rows name the same one
- route_gates: float32 [4096, 2], P(('groups', 'expert')), parts along dimension 0, may hold values from 0.2 to 1
- w_in: bfloat16 [16, 1024, 2048], P('expert', None, 'head'), may hold values from -0.1875 to 0.1875
- w_out: bfloat16 [16, 2048, 1024], P('expert', 'head'), may hold values from -0.09375 to 0.09375
- targets: bfloat16 [4096, 1024], P(('groups', 'expert')), parts along dimension 0, may hold values from -6 to 6
- dec_gain: float32 [1024], replicated, may hold values from 0.1 to 1.9
- src_lengths: int32 [64], P(('groups', 'expert')), parts along dimension 0, may hold values from 16 to 64, as said below
- tgt_lengths: int32 [64], P(('groups', 'expert')), parts along dimension 0, may hold values from 16 to 64, as said below
- w_query: bfloat16 [1024, 1024], P('expert', 'head'), may hold values from -60 to 60
- w_key: bfloat16 [1024, 1024], P('expert', 'head'), may hold values from -0.1875 to 0.1875
- w_value: bfloat16 [1024, 1024], P('expert', 'head'), may hold values from -0.1875 to 0.1875
- w_attn: bfloat16 [1024, 1024], P('expert', 'head'), may hold values from -0.1875 to 0.1875
Outputs:
- memory: bfloat16 [4096, 1024], P(('groups', 'expert')), parts along dimension 0
- decoded: bfloat16 [4096, 1024], P(('groups', 'expert'), 'head'), parts along dimension 0
The draws below stay inside these ranges and needn't reach their ends.
There are 2 independent parts, one for each index of `groups`. The reference program is written for one: setup_inputs(seed, part) draws one part's arguments, and reference() takes and returns one part's arrays. A program takes and returns all parts, laid end to end along the dimension named above; an argument that names none is the same for every part. Nothing has to cross between parts.
Inputs may be any that keep to these rules, and one draw needn't show every extreme that they name: `route_ids`: in each aligned block of 128 rows no expert is named more than 40 times, a bound that some block reaches. `src_lengths`: some sentence has exactly 64 live tokens. `tgt_lengths`: some sentence has exactly 64 live tokens.
All inputs are finite; a program needn't handle non-finite values.
Results may differ from the reference program's by a relative error of at most 0.025.
Values may be sent and summed in bfloat16 or wider, within the bound.
A program may use at most 64 MiB of HBM per device.

```python
import math
import jax
import jax.numpy as jnp
import numpy as np
from jax import lax

D = 1024
FF = 4096
HEADS = 16
DH = 64
EXPERTS = 8
SRC_LEN = 64
TGT_LEN = 64
SENT_DEV = 2
TOK_DEV = 128
CAP = 40
SENTS = 32
TOKENS = 2048
TGT_TOKENS = 2048
N_EXPERT = 16
N_HEAD = 1


def reach_lengths(key, longest):
    lengths = jax.random.randint(jax.random.fold_in(key, 11), (SENTS,), longest // 4, longest + 1)
    spot = jax.random.randint(jax.random.fold_in(key, 12), (), 0, SENTS)
    return jnp.where(jnp.arange(SENTS) == spot, longest, lengths).astype(jnp.int32)


def draw_src_lengths(key, part):
    return reach_lengths(jax.random.fold_in(key, 21), SRC_LEN)


def draw_tgt_lengths(key, part):
    return reach_lengths(jax.random.fold_in(key, 22), TGT_LEN)


def draw_w_query(key, part):
    base = jax.random.normal(jax.random.fold_in(key, 31), (D, D), jnp.float32)
    base = jnp.clip(base, -6.0, 6.0) * D ** (-0.5)
    return jnp.clip(base, -60.0, 60.0).astype(jnp.bfloat16)


def levels(stream_key, dims, shards, least, largest):
    level, own = 1.0, jax.random.fold_in(stream_key, 6)
    for dim, shards_of in shards:
        draws = jnp.exp(jax.random.uniform(jax.random.fold_in(own, dim), (shards_of,), jnp.float32, least / len(shards), largest / len(shards)))
        level = level * jnp.repeat(draws, dims[dim] // shards_of).reshape([-1 if axis == dim else 1 for axis in range(len(dims))])
    return level


def assign_block(stream_key, own, number, rows, amount, top, reach, slope):
    sequence = jax.random.permutation(stream_key, amount)
    crowded, ordinary = load_shares(amount, rows * top, reach, slope, True), load_shares(amount, rows * top, reach, slope, False)
    places = jnp.arange(amount)

    def named(sizes, rotation):
        used = int((sizes > 0).sum())
        fixed = max(1, used // 4)
        passed = fixed + (places - fixed + rotation * (used - fixed)) % max(1, amount - fixed)
        return jnp.zeros((amount,), jnp.int32).at[sequence[jnp.where(places < fixed, places, passed)]].set(jnp.asarray(sizes, jnp.int32))

    sizes = jnp.where(number % 4 == 0, named(crowded, number // 4), named(ordinary, number - number // 4 - 1))
    mixed = jax.random.permutation(jax.random.fold_in(own, 3), amount)
    giver, sink = mixed[0:amount // 2 * 2:2], mixed[1:amount // 2 * 2:2]
    room = jnp.minimum(sizes[giver] - 1, reach - sizes[sink]) // 2
    room = jnp.where((giver == sequence[0]) | (sink == sequence[0]) | (sizes[sink] == 0), 0, jnp.maximum(room, 0))
    passed = jax.random.randint(jax.random.fold_in(own, 4), (amount // 2,), 0, 1 << 20) % (room + 1)
    sizes = sizes.at[giver].add(-passed).at[sink].add(passed)
    labels = jnp.searchsorted(jnp.cumsum(sizes), jnp.arange(rows * top), side="right").astype(jnp.int32)
    grid = labels.reshape(top, rows).T
    grid = grid[jax.random.permutation(jax.random.fold_in(own, 1), rows)]
    rotation = jax.random.randint(jax.random.fold_in(own, 2), (rows, 1), 0, top)
    return jnp.take_along_axis(grid, (jnp.arange(top)[None, :] + rotation) % top, axis=1)


def load_shares(amount, total, reach, slope, full):
    portions = [(1 << 20) // math.isqrt(rank ** slope) + 1 for rank in range(1, amount + 1)]
    largest = reach if full else min(reach, max(-(-total // amount), total * portions[0] // sum(portions)))
    least = 1 if total - largest >= amount - 1 else 0
    holding, spare = [largest] + [least] * (amount - 1), total - largest - least * (amount - 1)
    while spare > 0:
        free = [i for i in range(1, amount) if holding[i] < largest] or [i for i in range(1, amount) if holding[i] < reach]
        pool, budget = sum([portions[i] for i in free]), spare
        for i in free:
            extra = min(reach - holding[i], max(1, budget * portions[i] // pool), spare)
            holding[i] = holding[i] + extra
            spare = spare - extra
    return np.array(holding)


def normal_values(own_key, dims, width, bound, shards=(), held_as=jnp.bfloat16):
    loudness = levels(own_key, dims, shards, -0.22, 0.18) if shards else 1.0
    result = jax.random.normal(own_key, dims, jnp.float32) * width * loudness
    return jnp.minimum(jnp.maximum(result, -bound), bound).astype(held_as)


def setup_inputs(seed: int = 0, part: int = 0) -> dict:
    arg_keys = jax.random.split(jax.random.key(seed), 15)
    part_splits = jax.random.split(jax.random.fold_in(arg_keys[14], part), 15)
    sources = normal_values(part_splits[0], (TOKENS, D), 1.0, 6.0, ((0, 16),))
    enc_gain = jnp.clip(1.0 + 0.18 * jax.random.normal(arg_keys[1], (D,), jnp.float32), 0.1, 1.9)
    route_ids_keys = jax.random.split(jax.random.fold_in(part_splits[2], 1), TOKENS // TOK_DEV)
    route_ids_turns = jax.random.permutation(jax.random.fold_in(part_splits[2], 3), TOKENS // TOK_DEV)
    route_ids = jax.vmap(lambda own, number: assign_block(jax.random.fold_in(part_splits[2], 2), own, number, TOK_DEV, EXPERTS, 2, CAP, 1))(route_ids_keys, route_ids_turns).reshape((TOKENS, 2))
    route_gates = jnp.clip(0.2 + 0.8 * jax.random.uniform(part_splits[3], (TOKENS, 2), jnp.float32) ** levels(part_splits[3], (TOKENS, 2), ((0, 16),), -0.2, 0.2), 0.2, 1.0)
    w_in = normal_values(arg_keys[4], (N_EXPERT, D, FF // 2), D ** -0.5, 0.1875, ((0, 16),))
    w_out = normal_values(arg_keys[5], (N_EXPERT, FF // 2, D), FF ** -0.5, 0.09375, ((0, 16),))
    targets = normal_values(part_splits[6], (TGT_TOKENS, D), 1.0, 6.0, ((0, 16),))
    dec_gain = jnp.clip(1.0 + 0.18 * jax.random.normal(arg_keys[7], (D,), jnp.float32), 0.1, 1.9)
    src_lengths = draw_src_lengths(jax.random.fold_in(jax.random.fold_in(arg_keys[14], part), 71), part)
    tgt_lengths = draw_tgt_lengths(jax.random.fold_in(jax.random.fold_in(arg_keys[14], part), 71), part)
    w_query = draw_w_query(jax.random.fold_in(arg_keys[14], 71), part)
    w_key = normal_values(arg_keys[11], (D, D), D ** -0.5, 0.1875, ((0, 16),))
    w_value = normal_values(arg_keys[12], (D, D), D ** -0.5, 0.1875, ((0, 16),))
    w_attn = normal_values(arg_keys[13], (D, D), D ** -0.5, 0.1875, ((0, 16),))
    return {"sources": sources, "enc_gain": enc_gain, "route_ids": route_ids, "route_gates": route_gates, "w_in": w_in, "w_out": w_out, "targets": targets, "dec_gain": dec_gain, "src_lengths": src_lengths, "tgt_lengths": tgt_lengths, "w_query": w_query, "w_key": w_key, "w_value": w_value, "w_attn": w_attn}


def layer_norm(rows, gain):
    rows = rows.astype(jnp.float32)
    mean = lax.optimization_barrier(jnp.mean(rows, axis=-1, keepdims=True))
    centered = rows - mean
    spread = lax.optimization_barrier(jnp.mean(centered * centered, axis=-1, keepdims=True))
    return centered * lax.rsqrt(spread + 1e-05) * gain.astype(jnp.float32)

def round_keep(values):
    rounded = lax.optimization_barrier(values.astype(jnp.bfloat16))
    return rounded.astype(jnp.float32)

def reference(sources, enc_gain, route_ids, route_gates, w_in, w_out, targets, dec_gain, src_lengths, tgt_lengths, w_query, w_key, w_value, w_attn):
    normed = layer_norm(sources, enc_gain).astype(jnp.bfloat16)
    blocks = route_ids.reshape(N_EXPERT, TOK_DEV * 2)
    onehot = (blocks[:, :, None] == jnp.arange(EXPERTS, dtype=jnp.int32)[None, None, :]).astype(jnp.int32)
    earlier = jnp.cumsum(onehot, axis=1) - onehot
    slots = lax.optimization_barrier(jnp.sum(earlier * onehot, axis=2)).astype(jnp.int32).reshape(TOKENS, 2)
    rows_per = N_EXPERT * CAP
    source_block = (jnp.arange(TOKENS, dtype=jnp.int32) // TOK_DEV).astype(jnp.int32)
    place = (route_ids * rows_per + source_block[:, None] * CAP + slots).astype(jnp.int32)
    buffer = jnp.zeros((EXPERTS * rows_per, D), jnp.bfloat16)
    buffer = buffer.at[place.reshape(-1)].set(jnp.repeat(normed, 2, axis=0))
    buffer = buffer.reshape(EXPERTS, rows_per, D)
    piece_width = FF // (2 * N_HEAD)

    def one_expert(index):
        rows = lax.dynamic_index_in_dim(buffer, index, 0, keepdims=False)
        total = jnp.zeros((rows_per, D), jnp.float32)
        for side in range(2):
            first = lax.dynamic_index_in_dim(w_in, 2 * index + side, 0, keepdims=False)
            second = lax.dynamic_index_in_dim(w_out, 2 * index + side, 0, keepdims=False)
            half = jnp.zeros((rows_per, D), jnp.float32)
            for piece in range(N_HEAD):
                lower = piece * piece_width
                hidden = jnp.maximum(jnp.dot(rows, first[:, lower:lower + piece_width], preferred_element_type=jnp.float32), 0.0).astype(jnp.bfloat16)
                term = jnp.dot(hidden, second[lower:lower + piece_width, :], preferred_element_type=jnp.float32)
                half = half + round_keep(term)
            total = total + round_keep(half)
        return total.astype(jnp.bfloat16)
    expert_out = lax.map(one_expert, jnp.arange(EXPERTS, dtype=jnp.int32)).reshape(EXPERTS * rows_per, D)
    first_pick = jnp.take(expert_out, place[:, 0], axis=0).astype(jnp.float32)
    second_pick = jnp.take(expert_out, place[:, 1], axis=0).astype(jnp.float32)
    moe = route_gates[:, 0:1] * first_pick + route_gates[:, 1:2] * second_pick
    memory = (sources.astype(jnp.float32) + moe).astype(jnp.bfloat16)
    tnormed = layer_norm(targets, dec_gain).astype(jnp.bfloat16)
    query = jnp.dot(tnormed, w_query, preferred_element_type=jnp.float32).astype(jnp.bfloat16)
    key = jnp.dot(memory, w_key, preferred_element_type=jnp.float32).astype(jnp.bfloat16)
    value = jnp.dot(memory, w_value, preferred_element_type=jnp.float32).astype(jnp.bfloat16)
    query_blocks = query.reshape(N_EXPERT, SENT_DEV, TGT_LEN, HEADS, DH)
    key_blocks = key.reshape(N_EXPERT, SENT_DEV, SRC_LEN, HEADS, DH)
    value_blocks = value.reshape(N_EXPERT, SENT_DEV, SRC_LEN, HEADS, DH)
    length_blocks = src_lengths.reshape(N_EXPERT, SENT_DEV)
    scale = DH ** (-0.5)

    def attend(pieces):
        queries, keys, values, lengths = pieces
        scores = jnp.einsum('sqhd,skhd->shqk', queries.astype(jnp.float32), keys.astype(jnp.float32)) * scale
        live = jnp.arange(SRC_LEN, dtype=jnp.int32)[None, :] < lengths[:, None]
        scores = jnp.where(live[:, None, None, :], scores, -1e+30)
        top = lax.optimization_barrier(jnp.max(scores, axis=-1, keepdims=True))
        raised = jnp.exp(scores - top)
        weights = (raised / lax.optimization_barrier(jnp.sum(raised, axis=-1, keepdims=True))).astype(jnp.bfloat16)
        return jnp.einsum('shqk,skhd->sqhd', weights.astype(jnp.float32), values.astype(jnp.float32)).astype(jnp.bfloat16)
    context = lax.map(attend, (query_blocks, key_blocks, value_blocks, length_blocks)).reshape(TGT_TOKENS, D)
    attn = jnp.dot(context, w_attn.T, preferred_element_type=jnp.float32)
    positions = jnp.arange(TGT_TOKENS, dtype=jnp.int32)
    owner = (positions // TGT_LEN).astype(jnp.int32)
    live_rows = (positions % TGT_LEN < jnp.take(tgt_lengths, owner)).astype(jnp.float32)
    decoded = ((targets.astype(jnp.float32) + attn) * live_rows[:, None]).astype(jnp.bfloat16)
    return (memory, decoded)
```

```python
import jax
import jax.numpy as jnp
from jax import lax
from jax.experimental import pallas as pl
from jax.experimental.pallas import tpu as pltpu
from jax.sharding import PartitionSpec as P

DH = 64


def from_partner(x, axis, stride):
    return lax.ppermute(x, axis, [(i, i ^ 1 << stride) for i in range(lax.axis_size(axis))])


def layer_norm(rows, gain):
    rows = rows.astype(jnp.float32)
    mean = jnp.mean(rows, axis=-1, keepdims=True)
    centered = rows - mean
    spread = jnp.mean(centered * centered, axis=-1, keepdims=True)
    return centered * lax.rsqrt(spread + 1e-05) * gain


def partner(block):
    return from_partner(block, "expert", 0)


def shards(
    sources,
    enc_gain,
    route_ids,
    route_gates,
    w_in,
    w_out,
    targets,
    dec_gain,
    src_lengths,
    tgt_lengths,
    w_query,
    w_key,
    w_value,
    w_attn,
):
    tok_rows, width = sources.shape
    experts = lax.axis_size("expert") // 2
    capacity = 2 * ((5 * tok_rows + 4 * experts - 1) // (4 * experts))
    side = lax.axis_index("expert") % 2
    pair_ids = route_ids.reshape(-1)
    onehot = (pair_ids[:, None] == jnp.arange(experts, dtype=jnp.int32)[None, :]).astype(jnp.int32)
    earlier = jnp.cumsum(onehot, axis=0) - onehot
    slots = jnp.sum(earlier * onehot, axis=1)
    place = pair_ids * capacity + slots
    normed = layer_norm(sources, enc_gain).astype(jnp.bfloat16)
    outgoing = (
        jnp.zeros((experts * capacity, width), jnp.bfloat16)
        .at[place]
        .set(jnp.repeat(normed, 2, axis=0))
    )
    sending = outgoing.reshape(2 * experts, capacity // 2, width)
    arrived = lax.all_to_all(sending, "expert", split_axis=0, concat_axis=0, tiled=True)
    other = partner(arrived)
    lower = jnp.where(side == 0, arrived, other)
    upper = jnp.where(side == 0, other, arrived)
    arrived = jnp.concatenate((lower, upper), axis=1)
    expert_rows = arrived.reshape(-1, width)
    hidden = jnp.maximum(
        jnp.dot(expert_rows, w_in[0], preferred_element_type=jnp.float32), 0.0
    ).astype(jnp.bfloat16)
    quarter = jnp.dot(hidden, w_out[0], preferred_element_type=jnp.float32)
    half = lax.psum(quarter.astype(jnp.bfloat16), "head")
    kept = half.shape[1]
    half = half.reshape(2 * experts, capacity, kept)
    other_half = partner(half)
    merged = (half.astype(jnp.float32) + other_half.astype(jnp.float32)).astype(jnp.bfloat16)
    leaving = lax.dynamic_slice_in_dim(merged, side * (capacity // 2), capacity // 2, 1)
    returned = lax.all_to_all(leaving, "expert", split_axis=0, concat_axis=0, tiled=True)
    results = returned.reshape(-1, kept)
    picked = jnp.take(results, place, axis=0).astype(jnp.float32).reshape(tok_rows, 2, kept)
    moe = route_gates[:, 0:1] * picked[:, 0, :] + route_gates[:, 1:2] * picked[:, 1, :]
    memory = (sources.astype(jnp.float32) + moe).astype(jnp.bfloat16)
    w_q, w_k, w_v, w_o = (
        lax.all_gather(w_query, "expert", axis=0, tiled=True),
        lax.all_gather(w_key, "expert", axis=0, tiled=True),
        lax.all_gather(w_value, "expert", axis=0, tiled=True),
        lax.all_gather(w_attn, "expert", axis=0, tiled=True),
    )
    tnormed = layer_norm(targets, dec_gain).astype(jnp.bfloat16)
    query = jnp.dot(tnormed, w_q, preferred_element_type=jnp.float32).astype(jnp.bfloat16)
    key = jnp.dot(memory, w_k, preferred_element_type=jnp.float32).astype(jnp.bfloat16)
    value = jnp.dot(memory, w_v, preferred_element_type=jnp.float32).astype(jnp.bfloat16)
    sentences = src_lengths.shape[0]
    local_heads = query.shape[1] // DH
    queries = query.reshape(sentences, -1, local_heads, DH)
    keys = key.reshape(sentences, -1, local_heads, DH)
    values = value.reshape(sentences, -1, local_heads, DH)
    key_count = keys.shape[1]
    scores = jnp.einsum(
        "sqhd,skhd->shqk", queries, keys, preferred_element_type=jnp.float32
    ) * DH ** (-0.5)
    live = jnp.arange(key_count, dtype=jnp.int32)[None, :] < src_lengths[:, None]
    scores = jnp.where(live[:, None, None, :], scores, -1e30)
    top = jnp.max(scores, axis=-1, keepdims=True)
    raised = jnp.exp(scores - top)
    weights = (raised / jnp.sum(raised, axis=-1, keepdims=True)).astype(jnp.bfloat16)
    context = jnp.einsum(
        "shqk,skhd->sqhd", weights, values, preferred_element_type=jnp.float32
    ).astype(jnp.bfloat16)
    context = context.reshape(targets.shape[0], -1)
    partial_out = lax.dot_general(
        context, w_o, (((1,), (1,)), ((), ())), preferred_element_type=jnp.float32
    )
    attn = lax.psum_scatter(
        partial_out.astype(jnp.bfloat16), "head", scatter_dimension=1, tiled=True
    ).astype(jnp.float32)
    share = width // lax.axis_size("head")
    own_targets = lax.dynamic_slice_in_dim(
        targets, lax.axis_index("head") * share, share, 1
    ).astype(jnp.float32)
    per_sentence = targets.shape[0] // sentences
    positions = jnp.arange(targets.shape[0], dtype=jnp.int32)
    owner = positions // per_sentence
    live_rows = (positions % per_sentence < jnp.take(tgt_lengths, owner)).astype(jnp.float32)
    decoded = ((own_targets + attn) * live_rows[:, None]).astype(jnp.bfloat16)
    return (memory, decoded)


def fused_kernel(
    src_len, tgt_len, sources, enc_gain, ids, gates, w_in, w_out, targets, dec_gain,
    w_q, w_k, w_v, w_o, memory, decoded,
    win, wout, wb, send, rows, hid, away, inbox, own, merged, back, tn, mem, bias, qkv, ctx, give, take,
    loc_sem, pair_send, pair_recv, d_send, d_recv, c_send, c_recv,
    w_recv, y_recv, up_send, dn_send, x_send, y_send,
):
    f32, bf16 = jnp.float32, jnp.bfloat16
    peers = lax.axis_size("expert")
    groups = lax.axis_size("groups")
    me, g = lax.axis_index("expert"), lax.axis_index("groups")
    p, chip = lax.rem(me, 2), lax.div(me, 2)
    mate = chip * 2 + 1 - p
    chips = peers // 2
    nx = 2 if chips % 2 == 0 else 1
    nz = chips // nx
    x, z = lax.rem(chip, nx), lax.div(chip, nx)
    tok, width = sources.shape
    half = width // 2
    cap = send.shape[1] // chips
    shard = w_q.shape[0]
    split = 2 if groups == 2 else 1
    mats = 4 // split

    def remote(src, dst, ss, rs, dev):
        return pltpu.make_async_remote_copy(
            src_ref=src, dst_ref=dst, send_sem=ss, recv_sem=rs,
            device_id=dev, device_id_type=pl.DeviceIdType.MESH,
        )

    def dev_of(zz, xx):
        return {"expert": (zz * nx + xx) * 2 + p}

    weights = (w_q, w_k, w_v, w_o)
    in_copy = pltpu.make_async_copy(w_in.at[0], win, loc_sem.at[0])
    out_copy = pltpu.make_async_copy(w_out.at[0], wout, loc_sem.at[1])
    own_rows = pl.ds(pl.multiple_of(me * shard, 16), shard)
    w_copies = [
        pltpu.make_async_copy(
            w.at[:, pl.ds(pl.multiple_of(p * half, 128), half)], wb.at[i, own_rows, :], loc_sem.at[2 + i]
        )
        for i, w in enumerate(weights)
    ]
    for c in w_copies:
        c.start()
    in_copy.start()
    out_copy.start()

    barrier = pltpu.get_barrier_semaphore()
    for d in range(1, peers):
        pl.semaphore_signal(
            barrier, inc=1, device_id={"expert": lax.rem(me + d, peers)},
            device_id_type=pl.DeviceIdType.MESH,
        )
    if split == 2:
        pl.semaphore_signal(
            barrier, inc=1, device_id={"groups": 1 - g}, device_id_type=pl.DeviceIdType.MESH
        )

    eye = lax.broadcasted_iota(jnp.int32, (tok, chips), 1)
    first = ids[:, 0:1]
    second = ids[:, 1:2]
    one0 = (eye == first).astype(f32)
    one1 = (eye == second).astype(f32)
    lower = (
        lax.broadcasted_iota(jnp.int32, (tok, tok), 0) > lax.broadcasted_iota(jnp.int32, (tok, tok), 1)
    ).astype(f32).astype(bf16)
    earlier = jnp.dot(lower, (one0 + one1).astype(bf16), preferred_element_type=f32)
    slot0 = jnp.sum(earlier * one0, axis=1, keepdims=True).astype(jnp.int32)
    slot1 = jnp.sum(earlier * one1, axis=1, keepdims=True).astype(jnp.int32)
    place0 = first * cap + slot0
    place1 = second * cap + slot1
    col = lax.broadcasted_iota(jnp.int32, (tok, chips * cap), 1)
    hit0 = (col == place0).astype(f32)
    hit1 = (col == place1).astype(f32)
    gated = hit0 * gates[:, 0:1] + hit1 * gates[:, 1:2]
    gate_hi = gated.astype(bf16)
    gate_lo = (gated - gate_hi.astype(f32)).astype(bf16)
    pick = (hit0 + hit1).T.astype(bf16)
    normed = layer_norm(sources[...], enc_gain[...]).astype(bf16)
    for h in range(2):
        send[h] = jnp.dot(
            pick, normed[:, h * half:(h + 1) * half], preferred_element_type=f32
        ).astype(bf16)

    pl.semaphore_wait(barrier, peers - 1 + (split - 1))

    def slot_rows(i):
        return pl.ds(pl.multiple_of(i * cap, 16), cap)

    def dispatch(d):
        to = lax.rem(me + d, peers)
        return remote(
            send.at[lax.rem(to, 2), slot_rows(lax.div(to, 2)), :],
            rows.at[lax.rem(to, 2), slot_rows(me), :],
            d_send.at[d], d_recv.at[me], {"expert": to},
        )

    def w_pair(i):
        return remote(
            weights[i].at[:, pl.ds(pl.multiple_of((1 - p) * half, 128), half)], wb.at[i, own_rows, :],
            pair_send.at[i], pair_recv.at[i], {"expert": mate},
        )

    for i in range(4):
        w_pair(i).start()
    for d in range(1, peers):
        dispatch(d).start()
    self_rows = pltpu.make_async_copy(
        send.at[p, slot_rows(chip), :], rows.at[p, slot_rows(me), :], loc_sem.at[6]
    )
    self_rows.start()

    def blk(c, gg):
        return wb.at[pl.ds(gg * mats, mats), pl.ds(pl.multiple_of(c * 2 * shard, 16), 2 * shard), :]

    gw = g if split == 2 else 0

    def w_up(zz):
        c = zz * nx + x
        return remote(blk(c, gw), blk(c, gw), up_send.at[zz], w_recv.at[c], dev_of(z + 1, x))

    def w_dn(zz):
        c = zz * nx + x
        return remote(blk(c, gw), blk(c, gw), dn_send.at[zz], w_recv.at[c], dev_of(z - 1, x))

    def w_x(zz):
        c = zz * nx + x
        return remote(blk(c, gw), blk(c, gw), x_send.at[zz], w_recv.at[c], dev_of(z, 1 - x))

    def w_y(c):
        return remote(blk(c, gw), blk(c, gw), y_send.at[c], y_recv.at[c], {"groups": 1 - g})

    def w_got(c):
        remote(blk(c, gw), blk(c, gw), x_send.at[0], w_recv.at[c], dev_of(z, x)).wait_recv()

    for c in w_copies:
        c.wait()
    for i in range(4):
        remote(
            w_q.at[:, pl.ds(0, half)], wb.at[i, pl.ds(pl.multiple_of(mate * shard, 16), shard), :],
            pair_send.at[i], pair_recv.at[i], {"expert": mate},
        ).wait_recv()

    can_up, can_dn = z < nz - 1, z > 0
    pl.when(can_up)(lambda: w_up(z).start())
    pl.when(can_dn)(lambda: w_dn(z).start())
    if nx == 2:
        w_x(z).start()

    def relay(d):
        @pl.when(z >= d)
        def _():
            w_got((z - d) * nx + x)
            pl.when(can_up)(lambda: w_up(z - d).start())
            if nx == 2:
                w_x(z - d).start()
            if split == 2:
                w_y((z - d) * nx + x).start()

        @pl.when(z + d < nz)
        def _():
            w_got((z + d) * nx + x)
            pl.when(can_dn)(lambda: w_dn(z + d).start())
            if nx == 2:
                w_x(z + d).start()
            if split == 2:
                w_y((z + d) * nx + x).start()

    per = tok // src_len.shape[0]
    lane = lax.broadcasted_iota(jnp.int32, bias.shape[1:], 1)
    limit = jnp.zeros(bias.shape[1:], jnp.int32)
    for s in range(src_len.shape[0]):
        limit = jnp.where(lax.div(lane, per) == s, src_len[s], limit)
    bias[p] = jnp.where(lax.rem(lane, per) < limit, 0.0, -1e30).astype(f32)
    tn[p] = layer_norm(targets[...], dec_gain[...]).astype(bf16)
    tn_pair = remote(tn.at[p], tn.at[p], pair_send.at[4], pair_recv.at[4], {"expert": mate})
    bias_pair = remote(bias.at[p], bias.at[p], pair_send.at[5], pair_recv.at[5], {"expert": mate})
    tn_pair.start()
    bias_pair.start()

    self_rows.wait()
    for d in range(1, peers):
        frm = lax.rem(me + d, peers)
        remote(
            send.at[0, slot_rows(0), :], rows.at[p, slot_rows(frm), :], d_send.at[d], d_recv.at[frm], {"expert": mate}
        ).wait_recv()
    x_pair = remote(rows.at[p], rows.at[p], pair_send.at[6], pair_recv.at[6], {"expert": mate})
    x_pair.start()
    if nz > 1:
        relay(1)
    in_copy.wait()
    remote(rows.at[1 - p], rows.at[1 - p], pair_send.at[6], pair_recv.at[6], {"expert": mate}).wait_recv()

    ftile = 256

    def up(i, _):
        cols = pl.ds(pl.multiple_of(i * ftile, ftile), ftile)
        acc = jnp.dot(rows[0], win[0:half, cols], preferred_element_type=f32)
        acc += jnp.dot(rows[1], win[half:, cols], preferred_element_type=f32)
        hid[:, cols] = jnp.maximum(acc, 0.0).astype(bf16)
        return 0

    lax.fori_loop(0, win.shape[1] // ftile, up, 0)
    if nz > 2:
        relay(2)
    out_copy.wait()

    def down(dst, base):
        def body(i, _):
            o = pl.multiple_of(i * ftile, ftile)
            acc = jnp.dot(
                hid[...], wout[:, pl.ds(pl.multiple_of(base + o, ftile), ftile)], preferred_element_type=f32
            )
            dst[:, pl.ds(o, ftile)] = acc.astype(bf16)
            return 0

        lax.fori_loop(0, half // ftile, body, 0)

    down(away, (1 - p) * half)
    y_pair = remote(away, inbox, pair_send.at[7], pair_recv.at[7], {"expert": mate})
    y_pair.start()
    down(own, p * half)
    y_pair.wait_recv()
    merged[...] = (own[...].astype(f32) + inbox[...].astype(f32)).astype(bf16)

    def combine(d):
        to = lax.rem(me + d, peers)
        return remote(
            merged.at[slot_rows(to), :], back.at[p, slot_rows(chip), :], c_send.at[d], c_recv.at[me], {"expert": to}
        )

    for d in range(1, peers):
        combine(d).start()
    self_back = pltpu.make_async_copy(
        merged.at[slot_rows(me), :], back.at[p, slot_rows(chip), :], loc_sem.at[7]
    )
    self_back.start()
    for d in range(3, nz):
        relay(d)
    if nx == 2:
        for k in range(nz):
            w_got(k * nx + 1 - x)
            if split == 2:
                w_y(k * nx + 1 - x).start()
    self_back.wait()
    for d in range(1, peers):
        frm = lax.rem(me + d, peers)
        remote(
            merged.at[slot_rows(0), :], back.at[lax.rem(frm, 2), slot_rows(lax.div(frm, 2)), :],
            c_send.at[d], c_recv.at[frm], {"expert": mate},
        ).wait_recv()
    for h in range(2):
        cols = slice(h * half, (h + 1) * half)
        moe = jnp.dot(gate_hi, back[h], preferred_element_type=f32)
        moe += jnp.dot(gate_lo, back[h], preferred_element_type=f32)
        mem[p, :, cols] = (sources[:, cols].astype(f32) + moe).astype(bf16)
    m_pair = remote(mem.at[p], mem.at[p], pair_send.at[8], pair_recv.at[8], {"expert": mate})
    m_pair.start()
    memory[...] = mem[p]
    remote(tn.at[1 - p], tn.at[1 - p], pair_send.at[4], pair_recv.at[4], {"expert": mate}).wait_recv()
    remote(bias.at[1 - p], bias.at[1 - p], pair_send.at[5], pair_recv.at[5], {"expert": mate}).wait_recv()
    if split == 2:
        for c in range(1, chips):
            cc = lax.rem(chip + c, chips)
            remote(
                blk(cc, 1 - g), blk(cc, 1 - g), y_send.at[cc], y_recv.at[cc], {"groups": 1 - g}
            ).wait_recv()

    qkv[0] = jnp.dot(
        tn[...].reshape(2 * tok, width), wb[0], preferred_element_type=f32
    ).astype(bf16)
    remote(mem.at[1 - p], mem.at[1 - p], pair_send.at[8], pair_recv.at[8], {"expert": mate}).wait_recv()
    both = mem[...].reshape(2 * tok, width)
    for i in (1, 2):
        qkv[i] = jnp.dot(both, wb[i], preferred_element_type=f32).astype(bf16)

    r = lax.broadcasted_iota(jnp.int32, (2 * tok, tok), 0)
    k = lax.broadcasted_iota(jnp.int32, (2 * tok, tok), 1)
    same = lax.div(lax.rem(r, tok), per) == lax.div(k, per)
    left = lax.broadcasted_iota(jnp.int32, (tok, 2 * DH), 1) < DH
    for o in range(2):
        keep = jnp.where(same, jnp.broadcast_to(bias[o, 0:1, :], (2 * tok, tok)), -1e30)
        dead = keep < 0.0
        for hp in range(half // (2 * DH)):
            cols = slice(hp * 2 * DH, (hp + 1) * 2 * DH)
            rws = slice(o * tok, (o + 1) * tok)
            q2 = qkv[0, rws, cols]
            zero = jnp.zeros_like(q2)
            qs = jnp.concatenate((jnp.where(left, q2, zero), jnp.where(left, zero, q2)), axis=0)
            sc = lax.dot_general(
                qs, qkv[1, rws, cols], (((1,), (1,)), ((), ())), preferred_element_type=f32
            ) * DH ** (-0.5)
            sc = jnp.where(dead, -1e30, sc)
            top = jnp.max(sc, axis=-1, keepdims=True)
            raised = jnp.exp(sc - top)
            wts = (raised / jnp.sum(raised, axis=-1, keepdims=True)).astype(bf16)
            mixed = jnp.dot(wts, qkv[2, rws, cols], preferred_element_type=f32)
            ctx[o, :, cols] = jnp.where(left, mixed[:tok], mixed[tok:]).astype(bf16)

    def project(o):
        return lax.dot_general(
            ctx[o], wb[3], (((1,), (1,)), ((), ())), preferred_element_type=f32
        )

    give[...] = project(1 - p).astype(bf16)
    o_pair = remote(give, take, pair_send.at[9], pair_recv.at[9], {"expert": mate})
    o_pair.start()
    mine = project(p)
    pos = lax.broadcasted_iota(jnp.int32, (tok, width), 0)
    per_t = tok // tgt_len.shape[0]
    tlimit = jnp.zeros((tok, width), jnp.int32)
    for s in range(tgt_len.shape[0]):
        tlimit = jnp.where(lax.div(pos, per_t) == s, tgt_len[s], tlimit)
    live = lax.rem(pos, per_t) < tlimit
    o_pair.wait_recv()
    total = targets[...].astype(f32) + (mine + take[...].astype(f32))
    decoded[...] = jnp.where(live, total, 0.0).astype(bf16)

    for i in range(4):
        w_pair(i).wait_send()
    for c in (tn_pair, bias_pair, x_pair, y_pair, m_pair, o_pair):
        c.wait_send()
    for d in range(1, peers):
        dispatch(d).wait_send()
        combine(d).wait_send()
    pl.when(can_up)(lambda: w_up(z).wait_send())
    pl.when(can_dn)(lambda: w_dn(z).wait_send())
    if nx == 2:
        w_x(z).wait_send()
    for d in range(1, nz):
        @pl.when(z >= d)
        def _():
            pl.when(can_up)(lambda: w_up(z - d).wait_send())
            if nx == 2:
                w_x(z - d).wait_send()
            if split == 2:
                w_y((z - d) * nx + x).wait_send()

        @pl.when(z + d < nz)
        def _():
            pl.when(can_dn)(lambda: w_dn(z + d).wait_send())
            if nx == 2:
                w_x(z + d).wait_send()
            if split == 2:
                w_y((z + d) * nx + x).wait_send()
    if nx == 2 and split == 2:
        for k in range(nz):
            w_y(k * nx + 1 - x).wait_send()


def fused(
    sources, enc_gain, route_ids, route_gates, w_in, w_out, targets, dec_gain,
    src_lengths, tgt_lengths, w_query, w_key, w_value, w_attn,
):
    tok, width = sources.shape
    peers = lax.axis_size("expert")
    chips = peers // 2
    half = width // 2
    capacity = 2 * ((5 * tok + 4 * chips - 1) // (4 * chips))
    cap = (capacity + 15) // 16 * 16
    hidden = w_in.shape[2]
    bf16 = jnp.bfloat16
    vm, sm, anym = (
        pl.BlockSpec(memory_space=pltpu.VMEM),
        pl.BlockSpec(memory_space=pltpu.SMEM),
        pl.BlockSpec(memory_space=pl.ANY),
    )
    dma = pltpu.SemaphoreType.DMA
    return pl.pallas_call(
        fused_kernel,
        out_shape=(jax.ShapeDtypeStruct((tok, width), bf16),) * 2,
        in_specs=[sm, sm, vm, vm, vm, vm, anym, anym, vm, vm, anym, anym, anym, anym],
        out_specs=(vm, vm),
        scratch_shapes=[
            pltpu.VMEM((width, hidden), bf16),
            pltpu.VMEM((hidden, width), bf16),
            pltpu.VMEM((4, width, half), bf16),
            pltpu.VMEM((2, chips * cap, half), bf16),
            pltpu.VMEM((2, peers * cap, half), bf16),
            pltpu.VMEM((peers * cap, hidden), bf16),
            pltpu.VMEM((peers * cap, half), bf16),
            pltpu.VMEM((peers * cap, half), bf16),
            pltpu.VMEM((peers * cap, half), bf16),
            pltpu.VMEM((peers * cap, half), bf16),
            pltpu.VMEM((2, chips * cap, half), bf16),
            pltpu.VMEM((2, tok, width), bf16),
            pltpu.VMEM((2, tok, width), bf16),
            pltpu.VMEM((2, 8, tok), jnp.float32),
            pltpu.VMEM((3, 2 * tok, half), bf16),
            pltpu.VMEM((2, tok, half), bf16),
            pltpu.VMEM((tok, width), bf16),
            pltpu.VMEM((tok, width), bf16),
            dma((8,)), dma((10,)), dma((10,)),
            dma((peers,)), dma((peers,)), dma((peers,)), dma((peers,)),
            dma((chips,)), dma((chips,)), dma((chips,)), dma((chips,)), dma((chips,)), dma((chips,)),
        ],
        compiler_params=pltpu.CompilerParams(
            collective_id=0, has_side_effects=True, vmem_limit_bytes=56 * 1024 * 1024
        ),
    )(
        src_lengths, tgt_lengths, sources, enc_gain.reshape(1, -1), route_ids, route_gates,
        w_in, w_out, targets, dec_gain.reshape(1, -1), w_query, w_key, w_value, w_attn,
    )


def solution(mesh):
    placed = (
        P(("groups", "expert"), None),
        P(),
        P(("groups", "expert"), None),
        P(("groups", "expert"), None),
        P("expert", None, "head"),
        P("expert", "head", None),
        P(("groups", "expert"), None),
        P(),
        P(("groups", "expert")),
        P(("groups", "expert")),
        P("expert", "head"),
        P("expert", "head"),
        P("expert", "head"),
        P("expert", "head"),
    )
    body = fused if mesh.shape["head"] == 1 else shards
    return jax.shard_map(
        body,
        mesh=mesh,
        in_specs=placed,
        out_specs=(P(("groups", "expert"), None), P(("groups", "expert"), "head")),
        check_vma=False,
    )
```
